128 devices in a mesh: energy: 32 (over y, z_lo, x), mom: 4 (over z_hi, core).
Axes of the slice: x: 4, y: 4, z: 4 (z_hi: 2, z_lo: 2; z = z_hi * 2 + z_lo), core: 2. Of those that a mesh axis runs over, the one named last changes fastest.
Arguments:
- green_ret: float32 [4, 32, 2, 10, 128, 128], P('mom', 'energy'), may hold values from -0.3125 to 0.3125
- scatter_in: float32 [4, 32, 2, 10, 128, 128], P('mom', 'energy'), may hold values from -6 to 6
- screened: float32 [4, 32, 2, 163840], P(None, None, None, ('energy', 'mom')), may hold values from -6 to 6
- momentum_table: int32 [4, 4], replicated, may hold values from 0 to 3, each once within a row
- tile_list: int32 [10, 2], replicated, may hold values from 0 to 3, as said below
Outputs:
- sigma_lesser: float32 [4, 32, 2, 10, 128, 128], P('mom', 'energy')
The draws below stay inside these ranges and needn't reach their ends.
Inputs may be any that keep to these rules, and one draw needn't show every extreme that they name: `tile_list`: each of the 10 blocks (r, c) with |r - c| <= 1 of the 4 x 4 block grid appears in exactly one row; column 0 is the block row, column 1 the block column. `momentum_table`: each row holds every momentum index once.
All inputs are finite; a program needn't handle non-finite values.
Results may differ from the reference program's by a relative error of at most 0.0003.
Values sent between devices are 32-bit elements; how exact they have to be, the bound alone decides.
A program may use at most 384 MiB of HBM per device.

```python
import jax
import jax.numpy as jnp
from jax import lax

TILE = 128
NB = 4
KPTS = 4
NE = 32
NTILE = 10
ELEM = 163840


def draw_tile_list(key, part):
    diag_rows = jnp.arange(NB, dtype=jnp.int32)
    upper_rows = jnp.arange(NB - 1, dtype=jnp.int32)
    block_rows = jnp.concatenate([diag_rows, upper_rows, upper_rows + 1])
    block_cols = jnp.concatenate([diag_rows, upper_rows + 1, upper_rows])
    coords = jnp.stack([block_rows, block_cols], axis=1)
    shuffled = jax.random.permutation(jax.random.fold_in(key, 7), NTILE)
    return coords[shuffled].astype(jnp.int32)


def shard_levels(rng, shape, cuts, low, high):
    factor_of, own = 1.0, jax.random.fold_in(rng, 6)
    for dim, blocks in cuts:
        heights = jnp.exp(jax.random.uniform(jax.random.fold_in(own, dim), (blocks,), jnp.float32, low / len(cuts), high / len(cuts)))
        factor_of = factor_of * jnp.repeat(heights, shape[dim] // blocks).reshape([-1 if axis == dim else 1 for axis in range(len(shape))])
    return factor_of


def bell_draw(own_key, shape, scale, reach, split=(), held_as=jnp.bfloat16):
    result = scale * jax.random.normal(own_key, shape, jnp.float32)
    if split:
        result = result * shard_levels(own_key, shape, split, -0.22, 0.18)
    return jnp.clip(result, -reach, reach).astype(held_as)


def setup_inputs(seed: int = 0) -> dict:
    splits = jax.random.split(jax.random.key(seed), 6)
    return {
        "green_ret": bell_draw(splits[0], (KPTS, NE, 2, NTILE, TILE, TILE), (3 * TILE) ** -0.5, 0.3125, ((0, 4), (1, 32)), jnp.float32),
        "scatter_in": bell_draw(splits[1], (KPTS, NE, 2, NTILE, TILE, TILE), 1.0, 6.0, ((0, 4), (1, 32)), jnp.float32),
        "screened": bell_draw(splits[2], (KPTS, NE, 2, ELEM), 1.0, 6.0, ((3, 128),), jnp.float32),
        "momentum_table": jax.vmap(lambda own: jax.random.permutation(own, KPTS))(jax.random.split(splits[3], KPTS)).reshape((KPTS, KPTS)).astype(jnp.int32),
        "tile_list": draw_tile_list(jax.random.fold_in(splits[5], 71), 0),
    }


def canon_positions(tile_list, nblock):
    block_rows = tile_list[:, 0]
    block_cols = tile_list[:, 1]
    offsets = block_cols - block_rows
    canon_order = jnp.where(offsets == 0, block_rows, jnp.where(offsets == 1, nblock + block_rows, 2 * nblock - 1 + block_cols)).astype(jnp.int32)
    tile_count = tile_list.shape[0]
    positions = jnp.arange(tile_count, dtype=jnp.int32)
    matches = (canon_order[None, :] == positions[:, None]).astype(jnp.int32)
    canon_slot = lax.optimization_barrier(jnp.sum(matches * positions[None, :], axis=1)).astype(jnp.int32)
    return (canon_order, canon_slot)

def canon_index(i, j, nblock):
    if i == j:
        return i
    if j == i + 1:
        return nblock + i
    return 2 * nblock - 1 + j

def neighbours(i, nblock):
    return [m for m in (i - 1, i, i + 1) if 0 <= m < nblock]

def complex_mul(left, right, adjoint):
    form = 'eij,ekj->eik' if adjoint else 'eij,ejk->eik'
    rr = jnp.einsum(form, left[0], right[0], precision=lax.Precision.HIGHEST)
    ii = jnp.einsum(form, left[1], right[1], precision=lax.Precision.HIGHEST)
    ri = jnp.einsum(form, left[0], right[1], precision=lax.Precision.HIGHEST)
    ir = jnp.einsum(form, left[1], right[0], precision=lax.Precision.HIGHEST)
    if adjoint:
        return (rr + ii, ir - ri)
    return (rr - ii, ri + ir)

def born_tiles(green, scatter, nblock):

    def tile_of(source, i, j):
        index = canon_index(i, j, nblock)
        return (source[:, 0, index], source[:, 1, index])
    crossed = {}
    for i in range(nblock):
        for k in neighbours(i, nblock):
            left = tile_of(green, i, k)
            for m in neighbours(k, nblock):
                product_term = complex_mul(left, tile_of(scatter, k, m), False)
                if (i, m) in crossed:
                    before = crossed[i, m]
                    crossed[i, m] = (before[0] + product_term[0], before[1] + product_term[1])
                else:
                    crossed[i, m] = product_term
    coords = [(i, i) for i in range(nblock)] + [(i, i + 1) for i in range(nblock - 1)] + [(i + 1, i) for i in range(nblock - 1)]
    real_tiles = []
    imag_tiles = []
    for i, j in coords:
        total_re = None
        total_im = None
        for m in neighbours(j, nblock):
            product_term = complex_mul(crossed[i, m], tile_of(green, j, m), True)
            if total_re is None:
                total_re, total_im = product_term
            else:
                total_re = total_re + product_term[0]
                total_im = total_im + product_term[1]
        real_tiles.append(total_re)
        imag_tiles.append(total_im)
    return jnp.stack([jnp.stack(real_tiles, axis=1), jnp.stack(imag_tiles, axis=1)], axis=1)

def energy_conv(lesser, screened, momentum_table):
    blocks = 32
    span = ELEM // blocks
    scale = 1.0 / jnp.sqrt(jnp.float32(KPTS * NE))
    pieces = []
    for index in range(blocks):
        lower = index * span
        green_part = lesser[:, :, :, lower:lower + span]
        screen_part = screened[:, :, :, lower:lower + span]
        green_freq = jnp.fft.fft(green_part[:, :, 0] + 1j * green_part[:, :, 1], n=2 * NE, axis=1)
        screen_freq = jnp.fft.fft(screen_part[:, :, 0] + 1j * screen_part[:, :, 1], n=2 * NE, axis=1)
        picked = jnp.take(green_freq, momentum_table, axis=0)
        summed = lax.optimization_barrier(jnp.sum(picked * screen_freq[None], axis=1))
        back = jnp.fft.ifft(summed, axis=1)[:, :NE]
        pieces.append(jnp.stack([-scale * back.imag, scale * back.real], axis=2).astype(jnp.float32))
    return jnp.concatenate(pieces, axis=3)

def reference(green_ret, scatter_in, screened, momentum_table, tile_list):
    canon_order, canon_slot = canon_positions(tile_list, NB)
    lesser_all = []
    for k in range(KPTS):
        green_canon = jnp.take(green_ret[k], canon_slot, axis=2)
        scatter_canon = jnp.take(scatter_in[k], canon_slot, axis=2)
        tiles_canon = born_tiles(green_canon, scatter_canon, NB)
        lesser_all.append(jnp.take(tiles_canon, canon_order, axis=2).reshape((NE, 2, ELEM)))
    lesser = jnp.stack(lesser_all)
    sigma = energy_conv(lesser, screened, momentum_table)
    return sigma.reshape((KPTS, NE, 2, NTILE, TILE, TILE))
```

```python
import functools
import math

import jax
import jax.numpy as jnp
import numpy as np
from jax import lax
from jax.experimental import pallas as pl
from jax.experimental.pallas import tpu as pltpu
from jax.sharding import PartitionSpec as P

MESH = pl.DeviceIdType.MESH
TILE = 128
NB = 4
KPTS = 4
NE = 32
NTILE = 10
ROWS = NTILE * TILE
NF = 2 * NE
NDEV = KPTS * NE
PER = ROWS // NDEV
CHUNKS = 2
STEP = PER // CHUNKS
F32 = jnp.float32
BF16 = jnp.bfloat16


def canon(i, j):
    if i == j:
        return i
    if j == i + 1:
        return NB + i
    return 2 * NB - 1 + j


def near(i):
    return [m for m in (i - 1, i, i + 1) if 0 <= m < NB]


TILES = [(i, i) for i in range(NB)] + [(i, i + 1) for i in range(NB - 1)] + [(i + 1, i) for i in range(NB - 1)]
CROSS = [(i, m) for i in range(NB) for m in range(NB) if abs(i - m) <= 2]


def split(x):
    high = x.astype(BF16)
    return high, (x - high.astype(F32)).astype(BF16)


def split_np(x):
    high = x.astype(jnp.bfloat16)
    low = (x - high.astype(np.float64)).astype(jnp.bfloat16)
    return high, low


def tables():
    phase = 2.0 * np.pi * (np.outer(np.arange(NF), np.arange(NE)) % NF) / NF
    cos, sin = np.cos(phase), np.sin(phase)
    forward = np.block([[cos, sin], [-sin, cos]])
    high, low = split_np(forward)
    forward3 = np.concatenate([high, high, low], axis=1)
    scale = 1.0 / math.sqrt(KPTS * NE) / NF
    cos, sin = cos.T * scale, sin.T * scale
    back = np.block([[-sin, -cos], [cos, -sin]])
    high, low = split_np(back)
    back3 = np.block([[high, high], [low, np.zeros_like(low)]])
    return forward3, back3


def dot(a, b):
    return lax.dot_general(a, b, (((1,), (0,)), ((), ())), preferred_element_type=F32)


def dot_t(a, b):
    return lax.dot_general(a, b, (((1,), (1,)), ((), ())), preferred_element_type=F32)


def peer(i, e, m):
    d = lax.rem(e * KPTS + m + i, NDEV)
    return d // KPTS, lax.rem(d, KPTS)


def kernel(tiles, mtab, fwd, bwd, green, scat, screened, out,
           gw, sw, cross, xs, lesc, send, recv, vin, vf, lf, back,
           in_sem, own_sem, a_send, a_recv, b_send, b_recv):
    e, m = lax.axis_index("energy"), lax.axis_index("mom")
    me = e * KPTS + m
    slot_me = m * NE + e

    barrier = pltpu.get_barrier_semaphore()

    @pl.loop(1, NDEV)
    def _(i):
        de, dm = peer(i, e, m)
        pl.semaphore_signal(barrier, inc=1, device_id=(de, dm), device_id_type=MESH)

    loads = []
    for q in range(KPTS):
        for c in range(2):
            loads.append(pltpu.make_async_copy(screened.at[q, :, c, :], vin.at[q, c], in_sem.at[q * 2 + c]))
            loads[-1].start()

    order = []
    for t in range(NTILE):
        row, col = tiles[t, 0], tiles[t, 1]
        off = col - row
        order.append(jnp.where(off == 0, row, jnp.where(off == 1, NB + row, 2 * NB - 1 + col)))
    slot = []
    for p in range(NTILE):
        total = jnp.int32(0)
        for t in range(NTILE):
            total = jnp.where(order[t] == p, t, total)
        slot.append(total)

    for p in range(NTILE):
        s = slot[p]
        for src, dst, flip in ((green, gw, False), (scat, sw, True)):
            re, im = split(src[0, s]), split(src[1, s])
            for h in range(2):
                dst[p, h, 0:TILE, 0:TILE] = re[h]
                dst[p, h, 0:TILE, TILE:] = im[h]
                dst[p, h, TILE:, 0:TILE] = -im[h]
                dst[p, h, TILE:, TILE:] = re[h]

    started = set()
    for k, mm in TILES:
        rows = near(k)
        w = canon(k, mm)
        high = [gw[canon(i, k), 0, 0:TILE, :] for i in rows]
        low = [gw[canon(i, k), 1, 0:TILE, :] for i in rows]
        n = len(rows) * TILE
        r1 = dot(jnp.concatenate(high + low, axis=0), sw[w, 0])
        r2 = dot(jnp.concatenate(high, axis=0), sw[w, 1])
        total = r1[:n] + (r1[n:] + r2)
        for a, i in enumerate(rows):
            x = CROSS.index((i, mm))
            part = total[a * TILE:(a + 1) * TILE]
            if x in started:
                cross[x] = cross[x] + part
            else:
                cross[x] = part
                started.add(x)
    for x in range(len(CROSS)):
        high, low = split(cross[x])
        xs[x, 0] = high
        xs[x, 1] = low
    started = set()
    for j, mm in TILES:
        rows = near(j)
        w = canon(j, mm)
        high = [xs[CROSS.index((i, mm)), 0] for i in rows]
        low = [xs[CROSS.index((i, mm)), 1] for i in rows]
        n = len(rows) * TILE
        r1 = dot_t(jnp.concatenate(high + low, axis=0), gw[w, 0])
        r2 = dot_t(jnp.concatenate(high, axis=0), gw[w, 1])
        total = r1[:n] + (r1[n:] + r2)
        for a, i in enumerate(rows):
            p = canon(i, j)
            part = total[a * TILE:(a + 1) * TILE]
            if p in started:
                lesc[p] = lesc[p] + part
            else:
                lesc[p] = part
                started.add(p)
    for t in range(NTILE):
        tile = lesc[order[t]]
        send[0, t * TILE:(t + 1) * TILE, :] = tile[:, 0:TILE]
        send[1, t * TILE:(t + 1) * TILE, :] = tile[:, TILE:]

    pl.semaphore_wait(barrier, NDEV - 1)

    def part(ref, index, h):
        return ref.at[:, pl.ds(index * PER + h * STEP, STEP), :]

    def total_of(ref):
        return ref.at[:, pl.ds(0, (NDEV - 1) * STEP), :]

    own = []
    for h in range(CHUNKS):
        @pl.loop(1, NDEV)
        def _(i):
            de, dm = peer(i, e, m)
            pltpu.make_async_remote_copy(
                part(send, de * KPTS + dm, h), part(recv, slot_me, h), a_send.at[h], a_recv.at[h],
                device_id=(de, dm), device_id_type=MESH).start()

        own.append(pltpu.make_async_copy(part(send, me, h), part(recv, slot_me, h), own_sem.at[h]))
        own[-1].start()

    for copy in loads:
        copy.wait()

    def transform(pieces, dst, j, count):
        high, low = [], []
        for piece in pieces:
            a, b = split(piece)
            high.append(a)
            low.append(b)
        high, low = jnp.concatenate(high, axis=1), jnp.concatenate(low, axis=1)
        freq = dot(fwd[...], jnp.concatenate([high, low, high], axis=0))
        for k in range(count):
            dst[k, j] = freq[:, k * TILE:(k + 1) * TILE]

    for j in range(PER):
        lanes = slice(j * TILE, (j + 1) * TILE)
        transform([vin[q, :, :, lanes].reshape(2 * NE, TILE) for q in range(KPTS)], vf, j, KPTS)

    a_done = []
    b_done = []
    for h in range(CHUNKS):
        own[h].wait()
        pltpu.make_async_remote_copy(
            total_of(send), total_of(recv), a_send.at[h], a_recv.at[h], device_id=(e, m), device_id_type=MESH).wait_recv()
        for j in range(h * STEP, (h + 1) * STEP):
            pieces = []
            for k in range(KPTS):
                both = [recv[c, pl.ds(k * NE * PER + j, NE, stride=PER), :] for c in range(2)]
                pieces.append(jnp.concatenate(both, axis=0))
            transform(pieces, lf, j, KPTS)
            high, low = [], []
            for k in range(KPTS):
                sum_re = sum_im = None
                for q in range(KPTS):
                    left = lf[mtab[k, q], j]
                    right = vf[q, j]
                    lr, li, vr, vi = left[:NF], left[NF:], right[:NF], right[NF:]
                    re, im = lr * vr - li * vi, lr * vi + li * vr
                    sum_re = re if sum_re is None else sum_re + re
                    sum_im = im if sum_im is None else sum_im + im
                a, b = split(jnp.concatenate([sum_re, sum_im], axis=0))
                high.append(a)
                low.append(b)
            stacked = jnp.concatenate([jnp.concatenate(high, axis=1), jnp.concatenate(low, axis=1)], axis=0)
            res = dot(bwd[...], stacked)
            res = res[:2 * NE] + res[2 * NE:]
            for k in range(KPTS):
                for c in range(2):
                    back[c, pl.ds(k * NE * PER + j, NE, stride=PER), :] = res[c * NE:(c + 1) * NE, k * TILE:(k + 1) * TILE]

        @pl.loop(1, NDEV)
        def _(i):
            de, dm = peer(i, e, m)
            pltpu.make_async_remote_copy(
                part(back, dm * NE + de, h), part(out, me, h), b_send.at[h], b_recv.at[h],
                device_id=(de, dm), device_id_type=MESH).start()

        last = pltpu.make_async_copy(part(back, slot_me, h), part(out, me, h), own_sem.at[CHUNKS + h])
        last.start()
        b_done.append(last)

    for h in range(CHUNKS):
        b_done[h].wait()
        pltpu.make_async_remote_copy(
            total_of(send), total_of(recv), a_send.at[h], a_recv.at[h], device_id=(e, m), device_id_type=MESH).wait_send()
        pltpu.make_async_remote_copy(
            total_of(back), total_of(out), b_send.at[h], b_recv.at[h], device_id=(e, m), device_id_type=MESH).wait()


def on_device(green_ret, scatter_in, screened, momentum_table, tile_list, fwd, bwd):
    green = green_ret.reshape(2, NTILE, TILE, TILE)
    scat = scatter_in.reshape(2, NTILE, TILE, TILE)
    vmem = pl.BlockSpec(memory_space=pltpu.VMEM)
    smem = pl.BlockSpec(memory_space=pltpu.SMEM)
    hbm = pl.BlockSpec(memory_space=pl.ANY)
    dma = pltpu.SemaphoreType.DMA
    out = pl.pallas_call(
        kernel,
        out_shape=jax.ShapeDtypeStruct((2, ROWS, TILE), F32),
        in_specs=[smem, smem, vmem, vmem, vmem, vmem, hbm],
        out_specs=hbm,
        scratch_shapes=[
            pltpu.VMEM((NTILE, 2, 2 * TILE, 2 * TILE), BF16),
            pltpu.VMEM((NTILE, 2, 2 * TILE, 2 * TILE), BF16),
            pltpu.VMEM((len(CROSS), TILE, 2 * TILE), F32),
            pltpu.VMEM((len(CROSS), 2, TILE, 2 * TILE), BF16),
            pltpu.VMEM((NTILE, TILE, 2 * TILE), F32),
            pltpu.VMEM((2, ROWS, TILE), F32),
            pltpu.VMEM((2, ROWS, TILE), F32),
            pltpu.VMEM((KPTS, 2, NE, ROWS), F32),
            pltpu.VMEM((KPTS, PER, 2 * NF, TILE), F32),
            pltpu.VMEM((KPTS, PER, 2 * NF, TILE), F32),
            pltpu.VMEM((2, ROWS, TILE), F32),
            dma((2 * KPTS,)),
            dma((2 * CHUNKS,)),
            dma((CHUNKS,)),
            dma((CHUNKS,)),
            dma((CHUNKS,)),
            dma((CHUNKS,)),
        ],
        compiler_params=pltpu.CompilerParams(
            collective_id=0, has_side_effects=True, vmem_limit_bytes=60 * 1024 * 1024
        ),
        name="born_exchange",
    )(tile_list, momentum_table, fwd, bwd, green, scat, screened)
    return out.reshape(green_ret.shape)


def solution(mesh):
    forward, backward = tables()
    in_specs = (
        P("mom", "energy", None, None, None, None),
        P("mom", "energy", None, None, None, None),
        P(None, None, None, ("energy", "mom")),
        P(),
        P(),
        P(),
        P(),
    )
    out_specs = P("mom", "energy", None, None, None, None)
    step = jax.shard_map(
        on_device, mesh=mesh, in_specs=in_specs, out_specs=out_specs, check_vma=False
    )

    def run(green_ret, scatter_in, screened, momentum_table, tile_list):
        return step(
            green_ret, scatter_in, screened, momentum_table, tile_list,
            jnp.asarray(forward), jnp.asarray(backward),
        )

    return run
```

```python
import functools
import math

import jax
import jax.numpy as jnp
import numpy as np
from jax import lax
from jax.experimental import pallas as pl
from jax.experimental.pallas import tpu as pltpu
from jax.sharding import PartitionSpec as P

FLAT = pl.DeviceIdType.LOGICAL
TILE = 128
NB = 4
KPTS = 4
NE = 32
NTILE = 10
ROWS = NTILE * TILE
NF = 2 * NE
NDEV = KPTS * NE
PER = ROWS // NDEV
CHUNKS = 2
STEP = PER // CHUNKS
F32 = jnp.float32
BF16 = jnp.bfloat16


def canon(i, j):
    if i == j:
        return i
    if j == i + 1:
        return NB + i
    return 2 * NB - 1 + j


def near(i):
    return [m for m in (i - 1, i, i + 1) if 0 <= m < NB]


TILES = [(i, i) for i in range(NB)] + [(i, i + 1) for i in range(NB - 1)] + [(i + 1, i) for i in range(NB - 1)]
CROSS = [(i, m) for i in range(NB) for m in range(NB) if abs(i - m) <= 2]


def split(x):
    high = x.astype(BF16)
    return high, (x - high.astype(F32)).astype(BF16)


def split_np(x):
    high = x.astype(jnp.bfloat16)
    low = (x - high.astype(np.float64)).astype(jnp.bfloat16)
    return high, low


def tables():
    phase = 2.0 * np.pi * (np.outer(np.arange(NF), np.arange(NE)) % NF) / NF
    cos, sin = np.cos(phase), np.sin(phase)
    forward = np.block([[cos, sin], [-sin, cos]])
    high, low = split_np(forward)
    forward3 = np.concatenate([high, high, low], axis=1)
    scale = 1.0 / math.sqrt(KPTS * NE) / NF
    cos, sin = cos.T * scale, sin.T * scale
    back = np.block([[-sin, -cos], [cos, -sin]])
    high, low = split_np(back)
    back3 = np.block([[high, high], [low, np.zeros_like(low)]])
    return forward3, back3


def dot(a, b):
    return lax.dot_general(a, b, (((1,), (0,)), ((), ())), preferred_element_type=F32)


def dot_t(a, b):
    return lax.dot_general(a, b, (((1,), (1,)), ((), ())), preferred_element_type=F32)


def peer(i, me):
    return (me + i * 27) & (NDEV - 1)


def kernel(tiles, mtab, fwd, bwd, green_in, scat_in, screened, out,
           green, scat, gw, sw, cross, xs, lesc, send, recv, vin, vf, lf, back,
           tile_sem, in_sem, own_sem, a_send, a_recv, b_send, b_recv):
    e, m = lax.axis_index("energy"), lax.axis_index("mom")
    me = e * KPTS + m
    slot_me = m * NE + e

    first = [pltpu.make_async_copy(green_in, green, tile_sem.at[0]), pltpu.make_async_copy(scat_in, scat, tile_sem.at[1])]
    for copy in first:
        copy.start()
    barrier = pltpu.get_barrier_semaphore()

    @pl.loop(1, NDEV)
    def _(i):
        pl.semaphore_signal(barrier, inc=1, device_id=peer(i, me), device_id_type=FLAT)

    loads = []
    for q in range(KPTS):
        for c in range(2):
            loads.append(pltpu.make_async_copy(screened.at[q, :, c, :], vin.at[q, c], in_sem.at[q * 2 + c]))
            loads[-1].start()

    order = []
    for t in range(NTILE):
        row, col = tiles[0, t], tiles[1, t]
        off = col - row
        order.append(jnp.where(off == 0, row, jnp.where(off == 1, NB + row, 2 * NB - 1 + col)))
    slot = []
    for p in range(NTILE):
        total = jnp.int32(0)
        for t in range(NTILE):
            total = jnp.where(order[t] == p, t, total)
        slot.append(total)

    for copy in first:
        copy.wait()
    for p in range(NTILE):
        s = slot[p]
        for src, dst, flip in ((green, gw, False), (scat, sw, True)):
            re, im = split(src[0, s]), split(src[1, s])
            for h in range(2):
                dst[p, h, 0:TILE, 0:TILE] = re[h]
                dst[p, h, 0:TILE, TILE:] = im[h]
                dst[p, h, TILE:, 0:TILE] = -im[h]
                dst[p, h, TILE:, TILE:] = re[h]

    started = set()
    for k, mm in TILES:
        rows = near(k)
        w = canon(k, mm)
        high = [gw[canon(i, k), 0, 0:TILE, :] for i in rows]
        low = [gw[canon(i, k), 1, 0:TILE, :] for i in rows]
        n = len(rows) * TILE
        r1 = dot(jnp.concatenate(high + low, axis=0), sw[w, 0])
        r2 = dot(jnp.concatenate(high, axis=0), sw[w, 1])
        total = r1[:n] + (r1[n:] + r2)
        for a, i in enumerate(rows):
            x = CROSS.index((i, mm))
            part = total[a * TILE:(a + 1) * TILE]
            if x in started:
                cross[x] = cross[x] + part
            else:
                cross[x] = part
                started.add(x)
    for x in range(len(CROSS)):
        high, low = split(cross[x])
        xs[x, 0] = high
        xs[x, 1] = low
    started = set()
    for j, mm in TILES:
        rows = near(j)
        w = canon(j, mm)
        high = [xs[CROSS.index((i, mm)), 0] for i in rows]
        low = [xs[CROSS.index((i, mm)), 1] for i in rows]
        n = len(rows) * TILE
        r1 = dot_t(jnp.concatenate(high + low, axis=0), gw[w, 0])
        r2 = dot_t(jnp.concatenate(high, axis=0), gw[w, 1])
        total = r1[:n] + (r1[n:] + r2)
        for a, i in enumerate(rows):
            p = canon(i, j)
            part = total[a * TILE:(a + 1) * TILE]
            if p in started:
                lesc[p] = lesc[p] + part
            else:
                lesc[p] = part
                started.add(p)
    for t in range(NTILE):
        tile = lesc[order[t]]
        send[0, t * TILE:(t + 1) * TILE, :] = tile[:, 0:TILE]
        send[1, t * TILE:(t + 1) * TILE, :] = tile[:, TILE:]

    pl.semaphore_wait(barrier, NDEV - 1)

    def part(ref, index, h):
        return ref.at[:, pl.ds(index * PER + h * STEP, STEP), :]

    def total_of(ref):
        return ref.at[:, pl.ds(0, (NDEV - 1) * STEP), :]

    own = []
    for h in range(CHUNKS):
        @pl.loop(1, NDEV)
        def _(i):
            d = peer(i, me)
            pltpu.make_async_remote_copy(
                part(send, d, h), part(recv, slot_me, h), a_send.at[h], a_recv.at[h],
                device_id=d, device_id_type=FLAT).start()

        own.append(pltpu.make_async_copy(part(send, me, h), part(recv, slot_me, h), own_sem.at[h]))
        own[-1].start()

    for copy in loads:
        copy.wait()

    def transform(pieces, dst, j, count):
        high, low = [], []
        for piece in pieces:
            a, b = split(piece)
            high.append(a)
            low.append(b)
        high, low = jnp.concatenate(high, axis=1), jnp.concatenate(low, axis=1)
        freq = dot(fwd[...], jnp.concatenate([high, low, high], axis=0))
        for k in range(count):
            dst[k, j] = freq[:, k * TILE:(k + 1) * TILE]

    for j in range(PER):
        lanes = slice(j * TILE, (j + 1) * TILE)
        transform([vin[q, :, :, lanes].reshape(2 * NE, TILE) for q in range(KPTS)], vf, j, KPTS)

    a_done = []
    b_done = []
    for h in range(CHUNKS):
        own[h].wait()
        pltpu.make_async_remote_copy(
            total_of(send), total_of(recv), a_send.at[h], a_recv.at[h], device_id=me, device_id_type=FLAT).wait_recv()
        for j in range(h * STEP, (h + 1) * STEP):
            pieces = []
            for k in range(KPTS):
                both = [recv[c, pl.ds(k * NE * PER + j, NE, stride=PER), :] for c in range(2)]
                pieces.append(jnp.concatenate(both, axis=0))
            transform(pieces, lf, j, KPTS)
            high, low = [], []
            for k in range(KPTS):
                sum_re = sum_im = None
                for q in range(KPTS):
                    left = lf[mtab[k, q], j]
                    right = vf[q, j]
                    lr, li, vr, vi = left[:NF], left[NF:], right[:NF], right[NF:]
                    re, im = lr * vr - li * vi, lr * vi + li * vr
                    sum_re = re if sum_re is None else sum_re + re
                    sum_im = im if sum_im is None else sum_im + im
                a, b = split(jnp.concatenate([sum_re, sum_im], axis=0))
                high.append(a)
                low.append(b)
            stacked = jnp.concatenate([jnp.concatenate(high, axis=1), jnp.concatenate(low, axis=1)], axis=0)
            res = dot(bwd[...], stacked)
            res = res[:2 * NE] + res[2 * NE:]
            for k in range(KPTS):
                for c in range(2):
                    back[c, pl.ds(k * NE * PER + j, NE, stride=PER), :] = res[c * NE:(c + 1) * NE, k * TILE:(k + 1) * TILE]

        @pl.loop(1, NDEV)
        def _(i):
            d = peer(i, me)
            pltpu.make_async_remote_copy(
                part(back, (d & (KPTS - 1)) * NE + (d >> 2), h), part(out, me, h), b_send.at[h], b_recv.at[h],
                device_id=d, device_id_type=FLAT).start()

        last = pltpu.make_async_copy(part(back, slot_me, h), part(out, me, h), own_sem.at[CHUNKS + h])
        last.start()
        b_done.append(last)

    for h in range(CHUNKS):
        b_done[h].wait()
        pltpu.make_async_remote_copy(
            total_of(send), total_of(recv), a_send.at[h], a_recv.at[h], device_id=me, device_id_type=FLAT).wait_send()
        pltpu.make_async_remote_copy(
            total_of(back), total_of(out), b_send.at[h], b_recv.at[h], device_id=me, device_id_type=FLAT).wait()


def on_device(green_ret, scatter_in, screened, momentum_table, tile_list, fwd, bwd):
    green = green_ret.reshape(2, NTILE, TILE, TILE)
    scat = scatter_in.reshape(2, NTILE, TILE, TILE)
    vmem = pl.BlockSpec(memory_space=pltpu.VMEM)
    smem = pl.BlockSpec(memory_space=pltpu.SMEM)
    hbm = pl.BlockSpec(memory_space=pl.ANY)
    dma = pltpu.SemaphoreType.DMA
    out = pl.pallas_call(
        kernel,
        out_shape=pltpu.VMEM((2, ROWS, TILE), F32),
        in_specs=[smem, smem, vmem, vmem, hbm, hbm, hbm],
        out_specs=vmem,
        scratch_shapes=[
            pltpu.VMEM((2, NTILE, TILE, TILE), F32),
            pltpu.VMEM((2, NTILE, TILE, TILE), F32),
            pltpu.VMEM((NTILE, 2, 2 * TILE, 2 * TILE), BF16),
            pltpu.VMEM((NTILE, 2, 2 * TILE, 2 * TILE), BF16),
            pltpu.VMEM((len(CROSS), TILE, 2 * TILE), F32),
            pltpu.VMEM((len(CROSS), 2, TILE, 2 * TILE), BF16),
            pltpu.VMEM((NTILE, TILE, 2 * TILE), F32),
            pltpu.VMEM((2, ROWS, TILE), F32),
            pltpu.VMEM((2, ROWS, TILE), F32),
            pltpu.VMEM((KPTS, 2, NE, ROWS), F32),
            pltpu.VMEM((KPTS, PER, 2 * NF, TILE), F32),
            pltpu.VMEM((KPTS, PER, 2 * NF, TILE), F32),
            pltpu.VMEM((2, ROWS, TILE), F32),
            dma((2,)),
            dma((2 * KPTS,)),
            dma((2 * CHUNKS,)),
            dma((CHUNKS,)),
            dma((CHUNKS,)),
            dma((CHUNKS,)),
            dma((CHUNKS,)),
        ],
        compiler_params=pltpu.CompilerParams(
            collective_id=0, has_side_effects=True, vmem_limit_bytes=60 * 1024 * 1024
        ),
        name="born_exchange",
    )(tile_list.T, momentum_table, fwd, bwd, green, scat, screened)
    return out.reshape(green_ret.shape)


def solution(mesh):
    forward, backward = tables()
    in_specs = (
        P("mom", "energy", None, None, None, None),
        P("mom", "energy", None, None, None, None),
        P(None, None, None, ("energy", "mom")),
        P(),
        P(),
        P(),
        P(),
    )
    out_specs = P("mom", "energy", None, None, None, None)
    step = jax.shard_map(
        on_device, mesh=mesh, in_specs=in_specs, out_specs=out_specs, check_vma=False
    )

    def run(green_ret, scatter_in, screened, momentum_table, tile_list):
        return step(
            green_ret, scatter_in, screened, momentum_table, tile_list,
            jnp.asarray(forward), jnp.asarray(backward),
        )

    return run
```

```python
import functools
import math

import jax
import jax.numpy as jnp
import numpy as np
from jax import lax
from jax.experimental import pallas as pl
from jax.experimental.pallas import tpu as pltpu
from jax.sharding import PartitionSpec as P

FLAT = pl.DeviceIdType.LOGICAL
TILE = 128
NB = 4
KPTS = 4
NE = 32
NTILE = 10
ROWS = NTILE * TILE
NF = 2 * NE
NDEV = KPTS * NE
PER = ROWS // NDEV
CHUNKS = 2
STEP = PER // CHUNKS
F32 = jnp.float32
BF16 = jnp.bfloat16


def canon(i, j):
    if i == j:
        return i
    if j == i + 1:
        return NB + i
    return 2 * NB - 1 + j


def near(i):
    return [m for m in (i - 1, i, i + 1) if 0 <= m < NB]


TILES = [(i, i) for i in range(NB)] + [(i, i + 1) for i in range(NB - 1)] + [(i + 1, i) for i in range(NB - 1)]
CROSS = [(i, m) for i in range(NB) for m in range(NB) if abs(i - m) <= 2]


def split(x):
    high = x.astype(BF16)
    return high, (x - high.astype(F32)).astype(BF16)


def split_np(x):
    high = x.astype(jnp.bfloat16)
    low = (x - high.astype(np.float64)).astype(jnp.bfloat16)
    return high, low


def tables():
    phase = 2.0 * np.pi * (np.outer(np.arange(NF), np.arange(NE)) % NF) / NF
    cos, sin = np.cos(phase), np.sin(phase)
    forward = np.block([[cos, sin], [-sin, cos]])
    high, low = split_np(forward)
    forward3 = np.concatenate([high, high, low], axis=1)
    scale = 1.0 / math.sqrt(KPTS * NE) / NF
    cos, sin = cos.T * scale, sin.T * scale
    back = np.block([[-sin, -cos], [cos, -sin]])
    high, low = split_np(back)
    back3 = np.block([[high, high], [low, np.zeros_like(low)]])
    return forward3, back3


def dot(a, b):
    return lax.dot_general(a, b, (((1,), (0,)), ((), ())), preferred_element_type=F32)


def dot_t(a, b):
    return lax.dot_general(a, b, (((1,), (1,)), ((), ())), preferred_element_type=F32)


def peer(i, me):
    return (me + i * 27) & (NDEV - 1)


def kernel(tiles, mtab, fwd, bwd, green_in, scat_in, screened, out,
           green, scat, gw, sw, cross, xs, lesc, send, recv, vin, vf, lf, back,
           tile_sem, in_sem, own_sem, a_send, a_recv, b_send, b_recv):
    e, m = lax.axis_index("energy"), lax.axis_index("mom")
    me = e * KPTS + m
    slot_me = m * NE + e

    first = [pltpu.make_async_copy(green_in, green, tile_sem.at[0]), pltpu.make_async_copy(scat_in, scat, tile_sem.at[1])]
    for copy in first:
        copy.start()
    barrier = pltpu.get_barrier_semaphore()

    @pl.loop(1, NDEV)
    def _(i):
        pl.semaphore_signal(barrier, inc=1, device_id=peer(i, me), device_id_type=FLAT)

    loads = []
    for q in range(KPTS):
        for c in range(2):
            loads.append(pltpu.make_async_copy(screened.at[q, :, c, :], vin.at[q, c], in_sem.at[q * 2 + c]))
            loads[-1].start()

    order = []
    for t in range(NTILE):
        row, col = tiles[0, t], tiles[1, t]
        off = col - row
        order.append(jnp.where(off == 0, row, jnp.where(off == 1, NB + row, 2 * NB - 1 + col)))
    slot = []
    for p in range(NTILE):
        total = jnp.int32(0)
        for t in range(NTILE):
            total = jnp.where(order[t] == p, t, total)
        slot.append(total)

    for copy in first:
        copy.wait()
    for p in range(NTILE):
        s = slot[p]
        for src, dst, flip in ((green, gw, False), (scat, sw, True)):
            re, im = split(src[0, s]), split(src[1, s])
            for h in range(2):
                dst[p, h, 0:TILE, 0:TILE] = re[h]
                dst[p, h, 0:TILE, TILE:] = im[h]
                dst[p, h, TILE:, 0:TILE] = -im[h]
                dst[p, h, TILE:, TILE:] = re[h]

    started = set()
    for k, mm in TILES:
        rows = near(k)
        w = canon(k, mm)
        high = [gw[canon(i, k), 0, 0:TILE, :] for i in rows]
        low = [gw[canon(i, k), 1, 0:TILE, :] for i in rows]
        n = len(rows) * TILE
        r1 = dot(jnp.concatenate(high + low, axis=0), sw[w, 0])
        r2 = dot(jnp.concatenate(high, axis=0), sw[w, 1])
        total = r1[:n] + (r1[n:] + r2)
        for a, i in enumerate(rows):
            x = CROSS.index((i, mm))
            part = total[a * TILE:(a + 1) * TILE]
            if x in started:
                cross[x] = cross[x] + part
            else:
                cross[x] = part
                started.add(x)
    for x in range(len(CROSS)):
        high, low = split(cross[x])
        xs[x, 0] = high
        xs[x, 1] = low
    started = set()
    for j, mm in TILES:
        rows = near(j)
        w = canon(j, mm)
        high = [xs[CROSS.index((i, mm)), 0] for i in rows]
        low = [xs[CROSS.index((i, mm)), 1] for i in rows]
        n = len(rows) * TILE
        r1 = dot_t(jnp.concatenate(high + low, axis=0), gw[w, 0])
        r2 = dot_t(jnp.concatenate(high, axis=0), gw[w, 1])
        total = r1[:n] + (r1[n:] + r2)
        for a, i in enumerate(rows):
            p = canon(i, j)
            part = total[a * TILE:(a + 1) * TILE]
            if p in started:
                lesc[p] = lesc[p] + part
            else:
                lesc[p] = part
                started.add(p)
    for t in range(NTILE):
        tile = lesc[order[t]]
        send[0, t * TILE:(t + 1) * TILE, :] = tile[:, 0:TILE]
        send[1, t * TILE:(t + 1) * TILE, :] = tile[:, TILE:]

    pl.semaphore_wait(barrier, NDEV - 1)

    def part(ref, index, h):
        return ref.at[:, pl.ds(index * PER + h * STEP, STEP), :]

    def total_of(ref):
        return ref.at[:, pl.ds(0, (NDEV - 1) * STEP), :]

    own = []
    for h in range(CHUNKS):
        @pl.loop(1, NDEV)
        def _(i):
            d = peer(i, me)
            pltpu.make_async_remote_copy(
                part(send, d, h), part(recv, slot_me, h), a_send.at[h], a_recv.at[h],
                device_id=d, device_id_type=FLAT).start()

        own.append(pltpu.make_async_copy(part(send, me, h), part(recv, slot_me, h), own_sem.at[h]))
        own[-1].start()

    for copy in loads:
        copy.wait()

    def transform(pieces, dst, j, count):
        high, low = [], []
        for piece in pieces:
            a, b = split(piece)
            high.append(a)
            low.append(b)
        high, low = jnp.concatenate(high, axis=1), jnp.concatenate(low, axis=1)
        freq = dot(fwd[...], jnp.concatenate([high, low, high], axis=0))
        for k in range(count):
            dst[k, j] = freq[:, k * TILE:(k + 1) * TILE]

    for j in range(PER):
        lanes = slice(j * TILE, (j + 1) * TILE)
        transform([vin[q, :, :, lanes].reshape(2 * NE, TILE) for q in range(KPTS)], vf, j, KPTS)

    a_done = []
    b_done = []
    for h in range(CHUNKS):
        own[h].wait()
        pltpu.make_async_remote_copy(
            total_of(send), total_of(recv), a_send.at[h], a_recv.at[h], device_id=me, device_id_type=FLAT).wait_recv()
        for j in range(h * STEP, (h + 1) * STEP):
            pieces = []
            for k in range(KPTS):
                both = [recv[c, pl.ds(k * NE * PER + j, NE, stride=PER), :] for c in range(2)]
                pieces.append(jnp.concatenate(both, axis=0))
            transform(pieces, lf, j, KPTS)
        for j in range(h * STEP, (h + 1) * STEP):
            high, low = [], []
            for k in range(KPTS):
                sum_re = sum_im = None
                for q in range(KPTS):
                    left = lf[mtab[k, q], j]
                    right = vf[q, j]
                    lr, li, vr, vi = left[:NF], left[NF:], right[:NF], right[NF:]
                    re, im = lr * vr - li * vi, lr * vi + li * vr
                    sum_re = re if sum_re is None else sum_re + re
                    sum_im = im if sum_im is None else sum_im + im
                a, b = split(jnp.concatenate([sum_re, sum_im], axis=0))
                high.append(a)
                low.append(b)
            stacked = jnp.concatenate([jnp.concatenate(high, axis=1), jnp.concatenate(low, axis=1)], axis=0)
            res = dot(bwd[...], stacked)
            res = res[:2 * NE] + res[2 * NE:]
            for k in range(KPTS):
                for c in range(2):
                    back[c, pl.ds(k * NE * PER + j, NE, stride=PER), :] = res[c * NE:(c + 1) * NE, k * TILE:(k + 1) * TILE]

        @pl.loop(1, NDEV)
        def _(i):
            d = peer(i, me)
            pltpu.make_async_remote_copy(
                part(back, (d & (KPTS - 1)) * NE + (d >> 2), h), part(out, me, h), b_send.at[h], b_recv.at[h],
                device_id=d, device_id_type=FLAT).start()

        last = pltpu.make_async_copy(part(back, slot_me, h), part(out, me, h), own_sem.at[CHUNKS + h])
        last.start()
        b_done.append(last)

    for h in range(CHUNKS):
        b_done[h].wait()
        pltpu.make_async_remote_copy(
            total_of(send), total_of(recv), a_send.at[h], a_recv.at[h], device_id=me, device_id_type=FLAT).wait_send()
        pltpu.make_async_remote_copy(
            total_of(back), total_of(out), b_send.at[h], b_recv.at[h], device_id=me, device_id_type=FLAT).wait()


def on_device(green_ret, scatter_in, screened, momentum_table, tile_list, fwd, bwd):
    green = green_ret.reshape(2, NTILE, TILE, TILE)
    scat = scatter_in.reshape(2, NTILE, TILE, TILE)
    vmem = pl.BlockSpec(memory_space=pltpu.VMEM)
    smem = pl.BlockSpec(memory_space=pltpu.SMEM)
    hbm = pl.BlockSpec(memory_space=pl.ANY)
    dma = pltpu.SemaphoreType.DMA
    out = pl.pallas_call(
        kernel,
        out_shape=pltpu.VMEM((2, ROWS, TILE), F32),
        in_specs=[smem, smem, vmem, vmem, hbm, hbm, hbm],
        out_specs=vmem,
        scratch_shapes=[
            pltpu.VMEM((2, NTILE, TILE, TILE), F32),
            pltpu.VMEM((2, NTILE, TILE, TILE), F32),
            pltpu.VMEM((NTILE, 2, 2 * TILE, 2 * TILE), BF16),
            pltpu.VMEM((NTILE, 2, 2 * TILE, 2 * TILE), BF16),
            pltpu.VMEM((len(CROSS), TILE, 2 * TILE), F32),
            pltpu.VMEM((len(CROSS), 2, TILE, 2 * TILE), BF16),
            pltpu.VMEM((NTILE, TILE, 2 * TILE), F32),
            pltpu.VMEM((2, ROWS, TILE), F32),
            pltpu.VMEM((2, ROWS, TILE), F32),
            pltpu.VMEM((KPTS, 2, NE, ROWS), F32),
            pltpu.VMEM((KPTS, PER, 2 * NF, TILE), F32),
            pltpu.VMEM((KPTS, PER, 2 * NF, TILE), F32),
            pltpu.VMEM((2, ROWS, TILE), F32),
            dma((2,)),
            dma((2 * KPTS,)),
            dma((2 * CHUNKS,)),
            dma((CHUNKS,)),
            dma((CHUNKS,)),
            dma((CHUNKS,)),
            dma((CHUNKS,)),
        ],
        compiler_params=pltpu.CompilerParams(
            collective_id=0, has_side_effects=True, vmem_limit_bytes=60 * 1024 * 1024
        ),
        name="born_exchange",
    )(tile_list.T, momentum_table, fwd, bwd, green, scat, screened)
    return out.reshape(green_ret.shape)


def solution(mesh):
    forward, backward = tables()
    in_specs = (
        P("mom", "energy", None, None, None, None),
        P("mom", "energy", None, None, None, None),
        P(None, None, None, ("energy", "mom")),
        P(),
        P(),
        P(),
        P(),
    )
    out_specs = P("mom", "energy", None, None, None, None)
    step = jax.shard_map(
        on_device, mesh=mesh, in_specs=in_specs, out_specs=out_specs, check_vma=False
    )

    def run(green_ret, scatter_in, screened, momentum_table, tile_list):
        return step(
            green_ret, scatter_in, screened, momentum_table, tile_list,
            jnp.asarray(forward), jnp.asarray(backward),
        )

    return run
```

```python
import functools
import math

import jax
import jax.numpy as jnp
import numpy as np
from jax import lax
from jax.experimental import pallas as pl
from jax.experimental.pallas import tpu as pltpu
from jax.sharding import PartitionSpec as P

FLAT = pl.DeviceIdType.LOGICAL
TILE = 128
NB = 4
KPTS = 4
NE = 32
NTILE = 10
ROWS = NTILE * TILE
NF = 2 * NE
NDEV = KPTS * NE
PER = ROWS // NDEV
CHUNKS = 2
STEP = PER // CHUNKS
F32 = jnp.float32
BF16 = jnp.bfloat16


def canon(i, j):
    if i == j:
        return i
    if j == i + 1:
        return NB + i
    return 2 * NB - 1 + j


def near(i):
    return [m for m in (i - 1, i, i + 1) if 0 <= m < NB]


TILES = [(i, i) for i in range(NB)] + [(i, i + 1) for i in range(NB - 1)] + [(i + 1, i) for i in range(NB - 1)]
CROSS = [(i, m) for i in range(NB) for m in range(NB) if abs(i - m) <= 2]


def split(x):
    high = x.astype(BF16)
    return high, (x - high.astype(F32)).astype(BF16)


def split_np(x):
    high = x.astype(jnp.bfloat16)
    low = (x - high.astype(np.float64)).astype(jnp.bfloat16)
    return high, low


def tables():
    phase = 2.0 * np.pi * (np.outer(np.arange(NF), np.arange(NE)) % NF) / NF
    cos, sin = np.cos(phase), np.sin(phase)
    forward = np.block([[cos, sin], [-sin, cos]])
    high, low = split_np(forward)
    forward3 = np.concatenate([high, high, low], axis=1)
    scale = 1.0 / math.sqrt(KPTS * NE) / NF
    cos, sin = cos.T * scale, sin.T * scale
    back = np.block([[-sin, -cos], [cos, -sin]])
    high, low = split_np(back)
    back3 = np.block([[high, high], [low, np.zeros_like(low)]])
    return forward3, back3


def dot(a, b):
    return lax.dot_general(a, b, (((1,), (0,)), ((), ())), preferred_element_type=F32)


def dot_t(a, b):
    return lax.dot_general(a, b, (((1,), (1,)), ((), ())), preferred_element_type=F32)


def peer(i, me, stride=27):
    return (me + i * stride) & (NDEV - 1)


def kernel(tiles, mtab, fwd, bwd, green_in, scat_in, screened, out,
           green, scat, gw, sw, cross, xs, lesc, send, recv, vin, vf, lf, back,
           tile_sem, in_sem, own_sem, a_send, a_recv, b_send, b_recv):
    e, m = lax.axis_index("energy"), lax.axis_index("mom")
    me = e * KPTS + m
    slot_me = m * NE + e

    first = [pltpu.make_async_copy(green_in, green, tile_sem.at[0]), pltpu.make_async_copy(scat_in, scat, tile_sem.at[1])]
    for copy in first:
        copy.start()
    barrier = pltpu.get_barrier_semaphore()

    for i in range(1, NDEV):
        pl.semaphore_signal(barrier, inc=1, device_id=peer(i, me), device_id_type=FLAT)

    loads = []
    for q in range(KPTS):
        for c in range(2):
            loads.append(pltpu.make_async_copy(screened.at[q, :, c, :], vin.at[q, c], in_sem.at[q * 2 + c]))
            loads[-1].start()

    order = []
    for t in range(NTILE):
        row, col = tiles[0, t], tiles[1, t]
        off = col - row
        order.append(jnp.where(off == 0, row, jnp.where(off == 1, NB + row, 2 * NB - 1 + col)))
    slot = []
    for p in range(NTILE):
        total = jnp.int32(0)
        for t in range(NTILE):
            total = jnp.where(order[t] == p, t, total)
        slot.append(total)

    for copy in first:
        copy.wait()
    for p in range(NTILE):
        s = slot[p]
        for src, dst, flip in ((green, gw, False), (scat, sw, True)):
            re, im = split(src[0, s]), split(src[1, s])
            for h in range(2):
                dst[p, h, 0:TILE, 0:TILE] = re[h]
                dst[p, h, 0:TILE, TILE:] = im[h]
                dst[p, h, TILE:, 0:TILE] = -im[h]
                dst[p, h, TILE:, TILE:] = re[h]

    started = set()
    for k, mm in TILES:
        rows = near(k)
        w = canon(k, mm)
        high = [gw[canon(i, k), 0, 0:TILE, :] for i in rows]
        low = [gw[canon(i, k), 1, 0:TILE, :] for i in rows]
        n = len(rows) * TILE
        r1 = dot(jnp.concatenate(high + low, axis=0), sw[w, 0])
        r2 = dot(jnp.concatenate(high, axis=0), sw[w, 1])
        total = r1[:n] + (r1[n:] + r2)
        for a, i in enumerate(rows):
            x = CROSS.index((i, mm))
            part = total[a * TILE:(a + 1) * TILE]
            if x in started:
                cross[x] = cross[x] + part
            else:
                cross[x] = part
                started.add(x)
    for x in range(len(CROSS)):
        high, low = split(cross[x])
        xs[x, 0] = high
        xs[x, 1] = low
    started = set()
    for j, mm in TILES:
        rows = near(j)
        w = canon(j, mm)
        high = [xs[CROSS.index((i, mm)), 0] for i in rows]
        low = [xs[CROSS.index((i, mm)), 1] for i in rows]
        n = len(rows) * TILE
        r1 = dot_t(jnp.concatenate(high + low, axis=0), gw[w, 0])
        r2 = dot_t(jnp.concatenate(high, axis=0), gw[w, 1])
        total = r1[:n] + (r1[n:] + r2)
        for a, i in enumerate(rows):
            p = canon(i, j)
            part = total[a * TILE:(a + 1) * TILE]
            if p in started:
                lesc[p] = lesc[p] + part
            else:
                lesc[p] = part
                started.add(p)
    for t in range(NTILE):
        tile = lesc[order[t]]
        send[0, t * TILE:(t + 1) * TILE, :] = tile[:, 0:TILE]
        send[1, t * TILE:(t + 1) * TILE, :] = tile[:, TILE:]

    pl.semaphore_wait(barrier, NDEV - 1)

    def part(ref, index, h):
        return ref.at[:, pl.ds(index * PER + h * STEP, STEP), :]

    def total_of(ref):
        return ref.at[:, pl.ds(0, (NDEV - 1) * STEP), :]

    own = []
    for h in range(CHUNKS):
        @pl.loop(1, NDEV)
        def _(i):
            d = peer(i, me)
            pltpu.make_async_remote_copy(
                part(send, d, h), part(recv, slot_me, h), a_send.at[h], a_recv.at[h],
                device_id=d, device_id_type=FLAT).start()

        own.append(pltpu.make_async_copy(part(send, me, h), part(recv, slot_me, h), own_sem.at[h]))
        own[-1].start()

    for copy in loads:
        copy.wait()

    def transform(pieces, dst, j, count):
        high, low = [], []
        for piece in pieces:
            a, b = split(piece)
            high.append(a)
            low.append(b)
        high, low = jnp.concatenate(high, axis=1), jnp.concatenate(low, axis=1)
        freq = dot(fwd[...], jnp.concatenate([high, low, high], axis=0))
        for k in range(count):
            dst[k, j] = freq[:, k * TILE:(k + 1) * TILE]

    for j in range(PER):
        lanes = slice(j * TILE, (j + 1) * TILE)
        transform([vin[q, :, :, lanes].reshape(2 * NE, TILE) for q in range(KPTS)], vf, j, KPTS)

    a_done = []
    b_done = []
    for h in range(CHUNKS):
        own[h].wait()
        pltpu.make_async_remote_copy(
            total_of(send), total_of(recv), a_send.at[h], a_recv.at[h], device_id=me, device_id_type=FLAT).wait_recv()
        for j in range(h * STEP, (h + 1) * STEP):
            pieces = []
            for k in range(KPTS):
                both = [recv[c, pl.ds(k * NE * PER + j, NE, stride=PER), :] for c in range(2)]
                pieces.append(jnp.concatenate(both, axis=0))
            transform(pieces, lf, j, KPTS)
        for j in range(h * STEP, (h + 1) * STEP):
            high, low = [], []
            for k in range(KPTS):
                sum_re = sum_im = None
                for q in range(KPTS):
                    left = lf[mtab[k, q], j]
                    right = vf[q, j]
                    lr, li, vr, vi = left[:NF], left[NF:], right[:NF], right[NF:]
                    re, im = lr * vr - li * vi, lr * vi + li * vr
                    sum_re = re if sum_re is None else sum_re + re
                    sum_im = im if sum_im is None else sum_im + im
                a, b = split(jnp.concatenate([sum_re, sum_im], axis=0))
                high.append(a)
                low.append(b)
            stacked = jnp.concatenate([jnp.concatenate(high, axis=1), jnp.concatenate(low, axis=1)], axis=0)
            res = dot(bwd[...], stacked)
            res = res[:2 * NE] + res[2 * NE:]
            for k in range(KPTS):
                for c in range(2):
                    back[c, pl.ds(k * NE * PER + j, NE, stride=PER), :] = res[c * NE:(c + 1) * NE, k * TILE:(k + 1) * TILE]

        @pl.loop(1, NDEV)
        def _(i):
            d = peer(i, me, 59)
            pltpu.make_async_remote_copy(
                part(back, (d & (KPTS - 1)) * NE + (d >> 2), h), part(out, me, h), b_send.at[h], b_recv.at[h],
                device_id=d, device_id_type=FLAT).start()

        last = pltpu.make_async_copy(part(back, slot_me, h), part(out, me, h), own_sem.at[CHUNKS + h])
        last.start()
        b_done.append(last)

    for h in range(CHUNKS):
        b_done[h].wait()
        pltpu.make_async_remote_copy(
            total_of(send), total_of(recv), a_send.at[h], a_recv.at[h], device_id=me, device_id_type=FLAT).wait_send()
        pltpu.make_async_remote_copy(
            total_of(back), total_of(out), b_send.at[h], b_recv.at[h], device_id=me, device_id_type=FLAT).wait()


def on_device(green_ret, scatter_in, screened, momentum_table, tile_list, fwd, bwd):
    green = green_ret.reshape(2, NTILE, TILE, TILE)
    scat = scatter_in.reshape(2, NTILE, TILE, TILE)
    vmem = pl.BlockSpec(memory_space=pltpu.VMEM)
    smem = pl.BlockSpec(memory_space=pltpu.SMEM)
    hbm = pl.BlockSpec(memory_space=pl.ANY)
    dma = pltpu.SemaphoreType.DMA
    out = pl.pallas_call(
        kernel,
        out_shape=pltpu.VMEM((2, ROWS, TILE), F32),
        in_specs=[smem, smem, vmem, vmem, hbm, hbm, hbm],
        out_specs=vmem,
        scratch_shapes=[
            pltpu.VMEM((2, NTILE, TILE, TILE), F32),
            pltpu.VMEM((2, NTILE, TILE, TILE), F32),
            pltpu.VMEM((NTILE, 2, 2 * TILE, 2 * TILE), BF16),
            pltpu.VMEM((NTILE, 2, 2 * TILE, 2 * TILE), BF16),
            pltpu.VMEM((len(CROSS), TILE, 2 * TILE), F32),
            pltpu.VMEM((len(CROSS), 2, TILE, 2 * TILE), BF16),
            pltpu.VMEM((NTILE, TILE, 2 * TILE), F32),
            pltpu.VMEM((2, ROWS, TILE), F32),
            pltpu.VMEM((2, ROWS, TILE), F32),
            pltpu.VMEM((KPTS, 2, NE, ROWS), F32),
            pltpu.VMEM((KPTS, PER, 2 * NF, TILE), F32),
            pltpu.VMEM((KPTS, PER, 2 * NF, TILE), F32),
            pltpu.VMEM((2, ROWS, TILE), F32),
            dma((2,)),
            dma((2 * KPTS,)),
            dma((2 * CHUNKS,)),
            dma((CHUNKS,)),
            dma((CHUNKS,)),
            dma((CHUNKS,)),
            dma((CHUNKS,)),
        ],
        compiler_params=pltpu.CompilerParams(
            collective_id=0, has_side_effects=True, vmem_limit_bytes=60 * 1024 * 1024
        ),
        name="born_exchange",
    )(tile_list.T, momentum_table, fwd, bwd, green, scat, screened)
    return out.reshape(green_ret.shape)


def solution(mesh):
    forward, backward = tables()
    in_specs = (
        P("mom", "energy", None, None, None, None),
        P("mom", "energy", None, None, None, None),
        P(None, None, None, ("energy", "mom")),
        P(),
        P(),
        P(),
        P(),
    )
    out_specs = P("mom", "energy", None, None, None, None)
    step = jax.shard_map(
        on_device, mesh=mesh, in_specs=in_specs, out_specs=out_specs, check_vma=False
    )

    def run(green_ret, scatter_in, screened, momentum_table, tile_list):
        return step(
            green_ret, scatter_in, screened, momentum_table, tile_list,
            jnp.asarray(forward), jnp.asarray(backward),
        )

    return run
```
